32 devices in a mesh: groups: 2 (over x), tensor: 16 (over z, y, core).
Axes of the slice: x: 2, y: 2, z: 4, core: 2. Of those that a mesh axis runs over, the one named last changes fastest.
Arguments:
- activations: bfloat16 [256, 26624], P('groups', 'tensor'), parts along dimension 0, may hold values from -6 to 6
- rotation_small: float32 [52, 52], replicated, may hold values from -0.875 to 0.875
- down_weight: bfloat16 [26624, 8192], P('tensor'), may hold values from -0.0546875 to 0.0546875
Outputs:
- projected: bfloat16 [256, 8192], P('groups', 'tensor'), parts along dimension 0
The draws below stay inside these ranges and needn't reach their ends.
There are 2 independent parts, one for each index of `groups`. The reference program is written for one: setup_inputs(seed, part) draws one part's arguments, and reference() takes and returns one part's arrays. A program takes and returns all parts, laid end to end along the dimension named above; an argument that names none is the same for every part. Nothing has to cross between parts.
All inputs are finite; a program needn't handle non-finite values.
Results may differ from the reference program's by a relative error of at most 0.005.
Values sent between devices are 32-bit elements; how exact they have to be, the bound alone decides.
A program may use at most 128 MiB of HBM per device.

```python
import jax
import jax.numpy as jnp
from jax import lax

D = 8192
FF = 26624
BLOCK = 52
TOK = 128


def with_spikes(entries, rng, source, target, blocks, factor):
    def block_of(dim):
        return (jnp.arange(entries.shape[dim]) // (entries.shape[dim] // blocks)).reshape((-1,) + (1,) * (entries.ndim - 1 - dim))

    near = jax.random.permutation(rng, blocks)[block_of(target)]
    second = (block_of(target) + blocks // 2) % blocks
    return jnp.where((block_of(source) == near) | (block_of(source) == second), factor * entries, entries)


def block_scale(stream_key, dims, shards, smallest, top_value):
    level, own = 1.0, jax.random.fold_in(stream_key, 6)
    for axis_at, shards_of in shards:
        draws = jnp.exp(jax.random.uniform(jax.random.fold_in(own, axis_at), (shards_of,), jnp.float32, smallest / len(shards), top_value / len(shards)))
        level = level * jnp.repeat(draws, dims[axis_at] // shards_of).reshape([-1 if axis == axis_at else 1 for axis in range(len(dims))])
    return level


def bell_draw(key, extent, deviation, reach, pieces=(), kind=jnp.bfloat16):
    values = deviation * jax.random.normal(key, extent, jnp.float32)
    if pieces:
        values = values * block_scale(key, extent, pieces, -0.22, 0.18)
    return jnp.clip(values, -reach, reach).astype(kind)


def heavy_noise(own_key, extent, deviation, reach, pieces, heavy, kind=jnp.bfloat16):
    entries = deviation * jax.random.normal(own_key, extent, jnp.float32)
    if pieces:
        entries = entries * block_scale(own_key, extent, pieces, -0.22, 0.18)
    return jnp.clip(with_spikes(entries, jax.random.fold_in(own_key, 3), *heavy), -reach, reach).astype(kind)


def setup_inputs(seed: int = 0, part: int = 0) -> dict:
    arg_keys = jax.random.split(jax.random.key(seed), 4)
    part_keys = jax.random.split(jax.random.fold_in(arg_keys[3], part), 4)
    activations = bell_draw(part_keys[0], (TOK, FF), 1.0, 6.0, ((1, 16),))
    rotation_small = bell_draw(arg_keys[1], (BLOCK, BLOCK), BLOCK ** -0.5, 0.875, (), jnp.float32)
    down_weight = heavy_noise(arg_keys[2], (FF, D), FF ** -0.5, 0.0546875, ((0, 16),), (0, 1, 16, 2.0))
    return {"activations": activations, "rotation_small": rotation_small, "down_weight": down_weight}


def sylvester(order):
    index = jnp.arange(order, dtype=jnp.int32)
    common = jnp.zeros((order, order), jnp.int32)
    for place in range(max(order.bit_length(), 1)):
        common = common + ((index[:, None] >> place) & 1) * ((index[None, :] >> place) & 1)
    return (1 - 2 * (common % 2)).astype(jnp.float32)


def reference(activations, rotation_small, down_weight):
    power = FF // BLOCK
    values = activations.astype(jnp.float32).reshape(TOK, power, BLOCK)
    hadamard = sylvester(power)
    mixed = jnp.einsum("tpq,pa->taq", values, hadamard, precision=lax.Precision.HIGHEST)
    mixed = jnp.einsum("taq,qb->tab", mixed, rotation_small.astype(jnp.float32), precision=lax.Precision.HIGHEST)
    rotated = (mixed * (power ** -0.5)).reshape(TOK, FF).astype(jnp.bfloat16)
    return jnp.dot(rotated, down_weight, preferred_element_type=jnp.float32).astype(jnp.bfloat16)
```

```python
import functools

import jax
import jax.numpy as jnp
from jax import lax
from jax.experimental import pallas as pl
from jax.experimental.pallas import tpu as pltpu
from jax.sharding import PartitionSpec as P

LANES = 128
ROWS = 8
SPLIT = 2


def sylvester(order):
    index = jnp.arange(order, dtype=jnp.int32)
    common = jnp.zeros((order, order), jnp.int32)
    for place in range(max(order.bit_length(), 1)):
        common = common + (index[:, None] >> place & 1) * (index[None, :] >> place & 1)
    return (1 - 2 * (common % 2)).astype(jnp.float32)


def plain(activations, rotation_small, down_weight):
    tokens, local = activations.shape
    shards = lax.axis_size("tensor")
    span = local // rotation_small.shape[0]
    kronecker = jnp.kron(sylvester(span), rotation_small)
    factor = (span * shards) ** (-0.5)
    values = activations.astype(jnp.float32)
    gathered = lax.all_to_all(values, "tensor", split_axis=0, concat_axis=1, tiled=True)
    gathered = gathered.reshape(-1, shards, local)
    gathered = jnp.einsum(
        "rsl,su->rul", gathered, sylvester(shards), precision=lax.Precision.HIGHEST
    )
    gathered = jnp.dot(gathered.reshape(-1, local), kronecker, precision=lax.Precision.HIGHEST)
    gathered = gathered.reshape(-1, shards * local)
    returned = lax.all_to_all(gathered, "tensor", split_axis=1, concat_axis=0, tiled=True)
    rotated = (returned * factor).astype(jnp.bfloat16)
    summed = lax.psum_scatter(
        lax.dot_general(
            down_weight, rotated, (((0,), (1,)), ((), ())), preferred_element_type=jnp.float32
        ),
        "tensor",
        scatter_dimension=0,
        tiled=True,
    )
    return summed.T.astype(jnp.bfloat16)


def widths_of(tiles):
    chunks = min(4, tiles)
    sizes = [tiles // chunks] * chunks
    for extra in range(tiles % chunks):
        sizes[(1 + extra) % chunks] += 1
    return [size * LANES for size in sizes]


def ends_first(count):
    low, high, order = 0, count - 1, []
    while low <= high:
        order.append(high)
        if low < high:
            order.append(low)
        low, high = low + 1, high - 1
    return order


def fused(n, widths, act, small, w_hbm, out, w_v, acc, *rest):
    chunks = len(widths)
    own, got, mixed, back = (rest[i * chunks : (i + 1) * chunks] for i in range(4))
    (from_core, from_y, from_low, from_high, w_sem, s1, r1, s2, r2, sa, ra, sb, rb,
     su, ru, sd, rd) = rest[4 * chunks :]
    tokens, local = act.shape
    block = small.shape[0]
    width = acc.shape[2]
    rows = tokens // n
    part = tokens // SPLIT
    nz = n // 4
    me = lax.axis_index("tensor")
    z, y, c = me // 4, (me // 2) % 2, me % 2
    starts = [sum(widths[:j]) for j in range(chunks)]
    scale = (local // block * n) ** (-0.5)

    def w_copy(j):
        span = pl.ds(starts[j], widths[j])
        return pltpu.make_async_copy(w_hbm.at[span], w_v.at[span], w_sem.at[j])

    for j in range(chunks):
        w_copy(j).start()

    barrier = pltpu.get_barrier_semaphore()

    def greet(k, carry):
        pl.semaphore_signal(barrier, inc=1, device_id={"tensor": lax.rem(me + k, n)})
        return carry

    lax.fori_loop(1, n, greet, 0)

    def remote(src, dst, send, recv, to):
        return pltpu.make_async_remote_copy(
            src_ref=src, dst_ref=dst, send_sem=send, recv_sem=recv,
            device_id={"tensor": to}, device_id_type=pl.DeviceIdType.MESH,
        )

    def rows_of(rank):
        return pl.ds(pl.multiple_of(rank * rows, ROWS), rows)

    def out_copy(j, k):
        to = lax.rem(me + k, n)
        return remote(own[j].at[rows_of(to)], got[j].at[me], s1.at[j, k], r1.at[j, k], to)

    def back_copy(j, k):
        to = lax.rem(me + k, n)
        return remote(mixed[j].at[to], back[j].at[rows_of(me)], s2.at[j, k], r2.at[j, k], to)

    def each(action):
        def step(k, carry):
            action(k)
            return carry

        lax.fori_loop(1, n, step, 0)

    def split_index(index):
        whole = jnp.floor((index.astype(jnp.float32) + 0.5) * (1.0 / block))
        whole = whole.astype(jnp.int32)
        return whole, index - whole * block

    r = small[...]
    r_high = r.astype(jnp.bfloat16)
    r_low = (r - r_high.astype(jnp.float32)).astype(jnp.bfloat16)
    span = local // block

    def dot(a, b):
        return jnp.dot(a, b, preferred_element_type=jnp.float32)

    for j, w in enumerate(widths):
        col_p, col_q = split_index(lax.broadcasted_iota(jnp.int32, (block, w), 1) + starts[j])
        line = lax.broadcasted_iota(jnp.int32, (block, w), 0)
        pick = jnp.where(col_q == line, 1.0, 0.0).astype(jnp.bfloat16)
        right_high = dot(r_high, pick).astype(jnp.bfloat16)
        right_low = dot(r_low, pick).astype(jnp.bfloat16)
        odd = jnp.zeros_like(line)
        for place in range(span.bit_length()):
            odd = odd + ((line >> place) & 1) * ((col_p >> place) & 1)
        sign_right = jnp.where(line < span, (1 - 2 * (odd & 1)).astype(jnp.float32), 0.0)
        sign_right = sign_right.astype(jnp.bfloat16)
        own[j][...] = jnp.zeros_like(own[j])

        def build(i, carry):
            base = pl.multiple_of(i * LANES, LANES)
            row_p, row_q = split_index(lax.broadcasted_iota(jnp.int32, (LANES, block), 0) + base)
            lane = lax.broadcasted_iota(jnp.int32, (LANES, block), 1)
            left = jnp.where(row_q == lane, 1.0, 0.0).astype(jnp.bfloat16)
            sign = dot(jnp.where(row_p == lane, 1.0, 0.0).astype(jnp.bfloat16), sign_right)
            high = (dot(left, right_high) * sign).astype(jnp.bfloat16)
            low = (dot(left, right_low) * sign).astype(jnp.bfloat16)
            x = act[:, pl.ds(base, LANES)]
            own[j][...] += dot(x, high) + dot(x, low)
            return carry

        lax.fori_loop(0, local // LANES, build, 0)
        if j == 0:
            pl.semaphore_wait(barrier, n - 1)
        each(lambda k: out_copy(j, k).start())
        got[j][me] = own[j][rows_of(me), :]

    for j, w in enumerate(widths):
        each(lambda k: out_copy(j, k).wait_recv())
        for at in range(0, w, LANES):
            values = [got[j][s, :, at : at + LANES] for s in range(n)]
            stride = 1
            while stride < n:
                for low in range(n):
                    if not low & stride:
                        a, b = values[low], values[low + stride]
                        values[low], values[low + stride] = a + b, a - b
                stride *= 2
            for s in range(n):
                mixed[j][s, :, at : at + LANES] = values[s] * scale
        each(lambda k: back_copy(j, k).start())
        back[j][rows_of(me), :] = mixed[j][me]

    def product(j, t):
        columns = pl.ds(pl.multiple_of(t * width, LANES), width)
        weight = w_v[pl.ds(starts[j], widths[j]), columns]
        return dot(back[j][...].astype(jnp.bfloat16), weight)

    for j in range(chunks - 1):
        each(lambda k: back_copy(j, k).wait_recv())
        w_copy(j).wait()

        def tile(t, carry):
            if j == 0:
                acc[t] = product(j, t)
            else:
                acc[t] += product(j, t)
            return carry

        lax.fori_loop(0, n, tile, 0)

    last = chunks - 1
    each(lambda k: back_copy(last, k).wait_recv())
    w_copy(last).wait()

    order = ends_first(nz)
    slots = [(far, to) for far in (1, 0) for to in order]

    def owner(to, far, other):
        side = 1 - y if far else y
        return to * 4 + side * 2 + (1 - c if other else c)

    def core_copy(slot):
        far, to = slots[slot]
        return remote(acc.at[owner(to, far, 1)], from_core.at[slot], sa.at[slot], ra.at[slot],
                      me + 1 - 2 * c)

    def y_copy(to, h):
        return remote(acc.at[owner(to, 1, 0), pl.ds(h * part, part)], from_y.at[to, h],
                      sb.at[to, h], rb.at[to, h], me + 2 * (1 - 2 * y))

    def up_copy(to, h, t):
        return remote(acc.at[t, pl.ds(h * part, part)], from_low.at[to, h],
                      su.at[to, h], ru.at[to, h], lax.rem(me + 4, n))

    def down_copy(to, h, t):
        return remote(acc.at[t, pl.ds(h * part, part)], from_high.at[to, h],
                      sd.at[to, h], rd.at[to, h], lax.rem(me + n - 4, n))

    for slot, (far, to) in enumerate(slots):
        t = owner(to, far, 1)
        acc[t] += product(last, t)
        core_copy(slot).start()
    for slot, (far, to) in enumerate(slots):
        t = owner(to, far, 0)
        acc[t] += product(last, t)
        core_copy(slot).wait_recv()
        acc[t] += from_core[slot]
        if far:
            for h in range(SPLIT):
                y_copy(to, h).start()

    for to in order:
        t = owner(to, 0, 0)
        for h in range(SPLIT):
            piece = pl.ds(h * part, part)
            y_copy(to, h).wait_recv()
            acc[t, piece] += from_y[to, h]

            @pl.when(z < to)
            def _():
                @pl.when(z > 0)
                def _():
                    up_copy(to, h, t).wait_recv()
                    acc[t, piece] += from_low[to, h]

                up_copy(to, h, t).start()

            @pl.when(z > to)
            def _():
                @pl.when(z < nz - 1)
                def _():
                    down_copy(to, h, t).wait_recv()
                    acc[t, piece] += from_high[to, h]

                down_copy(to, h, t).start()

    for h in range(SPLIT):
        piece = pl.ds(h * part, part)

        @pl.when(z > 0)
        def _():
            up_copy(z, h, me).wait_recv()
            acc[me, piece] += from_low[z, h]

        @pl.when(z < nz - 1)
        def _():
            down_copy(z, h, me).wait_recv()
            acc[me, piece] += from_high[z, h]

        out[piece, :] = acc[me, piece].astype(out.dtype)

    for j in range(chunks):
        each(lambda k: out_copy(j, k).wait_send())
        each(lambda k: back_copy(j, k).wait_send())
    for slot in range(len(slots)):
        core_copy(slot).wait_send()
    for to in order:
        for h in range(SPLIT):
            y_copy(to, h).wait_send()
            t = owner(to, 0, 0)

            @pl.when(z < to)
            def _():
                up_copy(to, h, t).wait_send()

            @pl.when(z > to)
            def _():
                down_copy(to, h, t).wait_send()


def body(activations, rotation_small, down_weight):
    tokens, local = activations.shape
    n = lax.axis_size("tensor")
    features = down_weight.shape[1]
    block = rotation_small.shape[0]
    if n % 4 or block * block < local or tokens % (ROWS * n) or local % LANES or features % (LANES * n):
        return plain(activations, rotation_small, down_weight)
    widths = widths_of(local // LANES)
    chunks, width, nz, part = len(widths), features // n, n // 4, tokens // SPLIT
    rows = tokens // n
    f32 = jnp.float32
    dma = pltpu.SemaphoreType.DMA
    return pl.pallas_call(
        functools.partial(fused, n, widths),
        out_shape=jax.ShapeDtypeStruct((tokens, width), jnp.bfloat16),
        in_specs=[
            pl.BlockSpec(memory_space=pltpu.VMEM),
            pl.BlockSpec(memory_space=pltpu.VMEM),
            pl.BlockSpec(memory_space=pl.ANY),
        ],
        out_specs=pl.BlockSpec(memory_space=pltpu.VMEM),
        scratch_shapes=[
            pltpu.VMEM((local, features), jnp.bfloat16),
            pltpu.VMEM((n, tokens, width), f32),
            *[pltpu.VMEM((tokens, w), f32) for w in widths],
            *[pltpu.VMEM((n, rows, w), f32) for w in widths],
            *[pltpu.VMEM((n, rows, w), f32) for w in widths],
            *[pltpu.VMEM((tokens, w), f32) for w in widths],
            pltpu.VMEM((2 * nz, tokens, width), f32),
            pltpu.VMEM((nz, SPLIT, part, width), f32),
            pltpu.VMEM((nz, SPLIT, part, width), f32),
            pltpu.VMEM((nz, SPLIT, part, width), f32),
            dma((chunks,)),
            *[dma((chunks, n))] * 4,
            *[dma((2 * nz,))] * 2,
            *[dma((nz, SPLIT))] * 6,
        ],
        compiler_params=pltpu.CompilerParams(
            collective_id=0, has_side_effects=True, vmem_limit_bytes=60 * 2**20
        ),
    )(activations, rotation_small, down_weight)


def solution(mesh):
    placed = (P("groups", "tensor"), P(), P("tensor", None))
    return jax.shard_map(
        body, mesh=mesh, in_specs=placed, out_specs=P("groups", "tensor"), check_vma=False
    )
```

```python
import functools

import jax
import jax.numpy as jnp
from jax import lax
from jax.experimental import pallas as pl
from jax.experimental.pallas import tpu as pltpu
from jax.sharding import PartitionSpec as P

LANES = 128
ROWS = 8
SPLIT = 2


def sylvester(order):
    index = jnp.arange(order, dtype=jnp.int32)
    common = jnp.zeros((order, order), jnp.int32)
    for place in range(max(order.bit_length(), 1)):
        common = common + (index[:, None] >> place & 1) * (index[None, :] >> place & 1)
    return (1 - 2 * (common % 2)).astype(jnp.float32)


def plain(activations, rotation_small, down_weight):
    tokens, local = activations.shape
    shards = lax.axis_size("tensor")
    span = local // rotation_small.shape[0]
    kronecker = jnp.kron(sylvester(span), rotation_small)
    factor = (span * shards) ** (-0.5)
    values = activations.astype(jnp.float32)
    gathered = lax.all_to_all(values, "tensor", split_axis=0, concat_axis=1, tiled=True)
    gathered = gathered.reshape(-1, shards, local)
    gathered = jnp.einsum(
        "rsl,su->rul", gathered, sylvester(shards), precision=lax.Precision.HIGHEST
    )
    gathered = jnp.dot(gathered.reshape(-1, local), kronecker, precision=lax.Precision.HIGHEST)
    gathered = gathered.reshape(-1, shards * local)
    returned = lax.all_to_all(gathered, "tensor", split_axis=1, concat_axis=0, tiled=True)
    rotated = (returned * factor).astype(jnp.bfloat16)
    summed = lax.psum_scatter(
        lax.dot_general(
            down_weight, rotated, (((0,), (1,)), ((), ())), preferred_element_type=jnp.float32
        ),
        "tensor",
        scatter_dimension=0,
        tiled=True,
    )
    return summed.T.astype(jnp.bfloat16)


def widths_of(tiles):
    chunks = min(4, tiles)
    sizes = [tiles // chunks] * chunks
    for extra in range(tiles % chunks):
        sizes[(1 + extra) % chunks] += 1
    return [size * LANES for size in sizes]


def ends_first(count):
    low, high, order = 0, count - 1, []
    while low <= high:
        order.append(high)
        if low < high:
            order.append(low)
        low, high = low + 1, high - 1
    return order


def fused(n, widths, act, small, w_hbm, out, w_v, acc, pieced, own, *rest):
    chunks = len(widths)
    got, mixed, back = (rest[i * chunks : (i + 1) * chunks] for i in range(3))
    (from_core, from_y, from_low, from_high, w_sem, s1, r1, s2, r2, sa, ra, sb, rb,
     su, ru, sd, rd) = rest[3 * chunks :]
    tokens, local = act.shape
    block = small.shape[0]
    width = acc.shape[2]
    rows = tokens // n
    part = tokens // SPLIT
    nz = n // 4
    me = lax.axis_index("tensor")
    z, y, c = me // 4, (me // 2) % 2, me % 2
    starts = [sum(widths[:j]) for j in range(chunks)]
    scale = (local // block * n) ** (-0.5)

    def w_copy(j):
        span = pl.ds(starts[j], widths[j])
        return pltpu.make_async_copy(w_hbm.at[span], w_v.at[span], w_sem.at[j])

    for j in range(chunks):
        w_copy(j).start()

    barrier = pltpu.get_barrier_semaphore()

    def greet(k, carry):
        pl.semaphore_signal(barrier, inc=1, device_id={"tensor": lax.rem(me + k, n)})
        return carry

    lax.fori_loop(1, n, greet, 0)

    def remote(src, dst, send, recv, to):
        return pltpu.make_async_remote_copy(
            src_ref=src, dst_ref=dst, send_sem=send, recv_sem=recv,
            device_id={"tensor": to}, device_id_type=pl.DeviceIdType.MESH,
        )

    def rows_of(rank):
        return pl.ds(pl.multiple_of(rank * rows, ROWS), rows)

    def out_copy(j, k):
        to = lax.rem(me + k, n)
        return remote(own.at[rows_of(to), pl.ds(starts[j], widths[j])], got[j].at[me], s1.at[j, k], r1.at[j, k], to)

    def back_copy(j, k):
        to = lax.rem(me + k, n)
        return remote(mixed[j].at[to], back[j].at[rows_of(me)], s2.at[j, k], r2.at[j, k], to)

    def each(action):
        def step(k, carry):
            action(k)
            return carry

        lax.fori_loop(1, n, step, 0)

    def split_index(index):
        whole = jnp.floor((index.astype(jnp.float32) + 0.5) * (1.0 / block))
        whole = whole.astype(jnp.int32)
        return whole, index - whole * block

    r = small[...]
    r_high = r.astype(jnp.bfloat16)
    r_low = (r - r_high.astype(jnp.float32)).astype(jnp.bfloat16)
    span = local // block

    def dot(a, b):
        return jnp.dot(a, b, preferred_element_type=jnp.float32)

    pieces, _, pw = pieced.shape
    inner = span // pieces

    def grid_of(shape, dim):
        return split_index(lax.broadcasted_iota(jnp.int32, shape, dim))

    def one_hot(hit):
        return jnp.where(hit, 1.0, 0.0).astype(jnp.bfloat16)

    col_p, col_q = grid_of((block, pw), 1)
    line = lax.broadcasted_iota(jnp.int32, (block, pw), 0)
    pick = one_hot(col_q == line)
    odd = jnp.zeros_like(line)
    for place in range(inner.bit_length()):
        odd = odd + ((line >> place) & 1) * ((col_p >> place) & 1)
    sign_right = jnp.where(line < inner, (1 - 2 * (odd & 1)).astype(jnp.float32), 0.0)
    row_p, row_q = grid_of((pw, block), 0)
    lane = lax.broadcasted_iota(jnp.int32, (pw, block), 1)
    left = one_hot(row_q == lane)
    sign = dot(one_hot(row_p == lane), sign_right.astype(jnp.bfloat16))
    high = (dot(left, dot(r_high, pick).astype(jnp.bfloat16)) * sign).astype(jnp.bfloat16)
    low = (dot(left, dot(r_low, pick).astype(jnp.bfloat16)) * sign).astype(jnp.bfloat16)
    for i in range(pieces):
        x = act[:, i * pw : (i + 1) * pw]
        pieced[i] = dot(x, high) + dot(x, low)

    def butterfly(values):
        stride = 1
        while stride < len(values):
            for at in range(len(values)):
                if not at & stride:
                    a, b = values[at], values[at + stride]
                    values[at], values[at + stride] = a + b, a - b
            stride *= 2
        return values

    for at in range(0, tokens, ROWS):
        values = butterfly([pieced[i, at : at + ROWS, :] for i in range(pieces)])
        own[at : at + ROWS, :] = jnp.concatenate(values, axis=1)
    pl.semaphore_wait(barrier, n - 1)
    for j in range(chunks):
        each(lambda k: out_copy(j, k).start())
        got[j][me] = own[rows_of(me), pl.ds(starts[j], widths[j])]

    for j, w in enumerate(widths):
        each(lambda k: out_copy(j, k).wait_recv())
        for at in range(0, w, LANES):
            values = butterfly([got[j][s, :, at : at + LANES] for s in range(n)])
            for s in range(n):
                mixed[j][s, :, at : at + LANES] = values[s] * scale
        each(lambda k: back_copy(j, k).start())
        back[j][rows_of(me), :] = mixed[j][me]

    def product(j, t):
        columns = pl.ds(pl.multiple_of(t * width, LANES), width)
        weight = w_v[pl.ds(starts[j], widths[j]), columns]
        return dot(back[j][...].astype(jnp.bfloat16), weight)

    for j in range(chunks - 1):
        each(lambda k: back_copy(j, k).wait_recv())
        w_copy(j).wait()

        def tile(t, carry):
            if j == 0:
                acc[t] = product(j, t)
            else:
                acc[t] += product(j, t)
            return carry

        lax.fori_loop(0, n, tile, 0)

    last = chunks - 1
    each(lambda k: back_copy(last, k).wait_recv())
    w_copy(last).wait()

    order = ends_first(nz)
    slots = [(far, to) for far in (1, 0) for to in order]

    def owner(to, far, other):
        side = 1 - y if far else y
        return to * 4 + side * 2 + (1 - c if other else c)

    def core_copy(slot):
        far, to = slots[slot]
        return remote(acc.at[owner(to, far, 1)], from_core.at[slot], sa.at[slot], ra.at[slot],
                      me + 1 - 2 * c)

    def y_copy(to, h):
        return remote(acc.at[owner(to, 1, 0), pl.ds(h * part, part)], from_y.at[to, h],
                      sb.at[to, h], rb.at[to, h], me + 2 * (1 - 2 * y))

    def up_copy(to, h, t):
        return remote(acc.at[t, pl.ds(h * part, part)], from_low.at[to, h],
                      su.at[to, h], ru.at[to, h], lax.rem(me + 4, n))

    def down_copy(to, h, t):
        return remote(acc.at[t, pl.ds(h * part, part)], from_high.at[to, h],
                      sd.at[to, h], rd.at[to, h], lax.rem(me + n - 4, n))

    for slot, (far, to) in enumerate(slots):
        t = owner(to, far, 1)
        acc[t] += product(last, t)
        core_copy(slot).start()
    for slot, (far, to) in enumerate(slots):
        t = owner(to, far, 0)
        acc[t] += product(last, t)
        core_copy(slot).wait_recv()
        acc[t] += from_core[slot]
        if far:
            for h in range(SPLIT):
                y_copy(to, h).start()

    for to in order:
        t = owner(to, 0, 0)
        for h in range(SPLIT):
            piece = pl.ds(h * part, part)
            y_copy(to, h).wait_recv()
            acc[t, piece] += from_y[to, h]

            @pl.when(z < to)
            def _():
                @pl.when(z > 0)
                def _():
                    up_copy(to, h, t).wait_recv()
                    acc[t, piece] += from_low[to, h]

                up_copy(to, h, t).start()

            @pl.when(z > to)
            def _():
                @pl.when(z < nz - 1)
                def _():
                    down_copy(to, h, t).wait_recv()
                    acc[t, piece] += from_high[to, h]

                down_copy(to, h, t).start()

    for h in range(SPLIT):
        piece = pl.ds(h * part, part)

        @pl.when(z > 0)
        def _():
            up_copy(z, h, me).wait_recv()
            acc[me, piece] += from_low[z, h]

        @pl.when(z < nz - 1)
        def _():
            down_copy(z, h, me).wait_recv()
            acc[me, piece] += from_high[z, h]

        out[piece, :] = acc[me, piece].astype(out.dtype)

    for j in range(chunks):
        each(lambda k: out_copy(j, k).wait_send())
        each(lambda k: back_copy(j, k).wait_send())
    for slot in range(len(slots)):
        core_copy(slot).wait_send()
    for to in order:
        for h in range(SPLIT):
            y_copy(to, h).wait_send()
            t = owner(to, 0, 0)

            @pl.when(z < to)
            def _():
                up_copy(to, h, t).wait_send()

            @pl.when(z > to)
            def _():
                down_copy(to, h, t).wait_send()


def body(activations, rotation_small, down_weight):
    tokens, local = activations.shape
    n = lax.axis_size("tensor")
    features = down_weight.shape[1]
    block = rotation_small.shape[0]
    if n % 4 or block * block < local or tokens % (ROWS * n) or local % LANES or features % (LANES * n):
        return plain(activations, rotation_small, down_weight)
    widths = widths_of(local // LANES)
    chunks, width, nz, part = len(widths), features // n, n // 4, tokens // SPLIT
    rows = tokens // n
    pieces = 1
    while local // pieces > 2 * LANES and local // block % (2 * pieces) == 0:
        pieces *= 2
    f32 = jnp.float32
    dma = pltpu.SemaphoreType.DMA
    return pl.pallas_call(
        functools.partial(fused, n, widths),
        out_shape=jax.ShapeDtypeStruct((tokens, width), jnp.bfloat16),
        in_specs=[
            pl.BlockSpec(memory_space=pltpu.VMEM),
            pl.BlockSpec(memory_space=pltpu.VMEM),
            pl.BlockSpec(memory_space=pl.ANY),
        ],
        out_specs=pl.BlockSpec(memory_space=pltpu.VMEM),
        scratch_shapes=[
            pltpu.VMEM((local, features), jnp.bfloat16),
            pltpu.VMEM((n, tokens, width), f32),
            pltpu.VMEM((pieces, tokens, local // pieces), f32),
            pltpu.VMEM((tokens, local), f32),
            *[pltpu.VMEM((n, rows, w), f32) for w in widths],
            *[pltpu.VMEM((n, rows, w), f32) for w in widths],
            *[pltpu.VMEM((tokens, w), f32) for w in widths],
            pltpu.VMEM((2 * nz, tokens, width), f32),
            pltpu.VMEM((nz, SPLIT, part, width), f32),
            pltpu.VMEM((nz, SPLIT, part, width), f32),
            pltpu.VMEM((nz, SPLIT, part, width), f32),
            dma((chunks,)),
            *[dma((chunks, n))] * 4,
            *[dma((2 * nz,))] * 2,
            *[dma((nz, SPLIT))] * 6,
        ],
        compiler_params=pltpu.CompilerParams(
            collective_id=0, has_side_effects=True, vmem_limit_bytes=60 * 2**20
        ),
    )(activations, rotation_small, down_weight)


def solution(mesh):
    placed = (P("groups", "tensor"), P(), P("tensor", None))
    return jax.shard_map(
        body, mesh=mesh, in_specs=placed, out_specs=P("groups", "tensor"), check_vma=False
    )
```

```python
import functools

import jax
import jax.numpy as jnp
from jax import lax
from jax.experimental import pallas as pl
from jax.experimental.pallas import tpu as pltpu
from jax.sharding import PartitionSpec as P

LANES = 128
ROWS = 8
SPLIT = 2


def sylvester(order):
    index = jnp.arange(order, dtype=jnp.int32)
    common = jnp.zeros((order, order), jnp.int32)
    for place in range(max(order.bit_length(), 1)):
        common = common + (index[:, None] >> place & 1) * (index[None, :] >> place & 1)
    return (1 - 2 * (common % 2)).astype(jnp.float32)


def plain(activations, rotation_small, down_weight):
    tokens, local = activations.shape
    shards = lax.axis_size("tensor")
    span = local // rotation_small.shape[0]
    kronecker = jnp.kron(sylvester(span), rotation_small)
    factor = (span * shards) ** (-0.5)
    values = activations.astype(jnp.float32)
    gathered = lax.all_to_all(values, "tensor", split_axis=0, concat_axis=1, tiled=True)
    gathered = gathered.reshape(-1, shards, local)
    gathered = jnp.einsum(
        "rsl,su->rul", gathered, sylvester(shards), precision=lax.Precision.HIGHEST
    )
    gathered = jnp.dot(gathered.reshape(-1, local), kronecker, precision=lax.Precision.HIGHEST)
    gathered = gathered.reshape(-1, shards * local)
    returned = lax.all_to_all(gathered, "tensor", split_axis=1, concat_axis=0, tiled=True)
    rotated = (returned * factor).astype(jnp.bfloat16)
    summed = lax.psum_scatter(
        lax.dot_general(
            down_weight, rotated, (((0,), (1,)), ((), ())), preferred_element_type=jnp.float32
        ),
        "tensor",
        scatter_dimension=0,
        tiled=True,
    )
    return summed.T.astype(jnp.bfloat16)


def ends_first(count):
    low, high, order = 0, count - 1, []
    while low <= high:
        order.append(high)
        if low < high:
            order.append(low)
        low, high = low + 1, high - 1
    return order


def fused(n, act, small, w_hbm, out, w_v, acc, pieced, own, got, mixed, back, rotated, from_core,
          from_y, from_low, from_high, w_sem, s1, r1, s2, r2, sa, ra, sb, rb, su, ru, sd, rd):
    tokens, local = act.shape
    block = small.shape[0]
    width = acc.shape[3]
    part = tokens // SPLIT
    rows = part // (n // 2)
    wide = got.shape[3]
    shift = local - wide
    nz = n // 4
    me = lax.axis_index("tensor")
    z, y, c = me // 4, (me // 2) % 2, me % 2
    scale = (local // block * n) ** (-0.5)
    w_copy = pltpu.make_async_copy(w_hbm, w_v, w_sem)
    w_copy.start()

    barrier = pltpu.get_barrier_semaphore()

    def greet(k, carry):
        pl.semaphore_signal(barrier, inc=1, device_id={"tensor": lax.rem(me + k, n)})
        return carry

    lax.fori_loop(1, n, greet, 0)

    def remote(src, dst, send, recv, to):
        return pltpu.make_async_remote_copy(
            src_ref=src, dst_ref=dst, send_sem=send, recv_sem=recv,
            device_id={"tensor": to}, device_id_type=pl.DeviceIdType.MESH,
        )

    def rows_of(rank, base=0):
        return pl.ds(pl.multiple_of(base + rank // 2 * rows, ROWS), rows)

    def columns_of(rank):
        return pl.ds(pl.multiple_of(rank % 2 * shift, LANES), wide)

    def out_copy(h, k):
        to = lax.rem(me + k, n)
        return remote(own.at[rows_of(to, h * part), columns_of(to)], got.at[h, me],
                      s1.at[h, k], r1.at[h, k], to)

    def back_copy(h, k):
        to = lax.rem(me + k, n)
        return remote(mixed.at[h, to], back.at[h, c, rows_of(me)], s2.at[h, k], r2.at[h, k], to)

    def each(action):
        def step(k, carry):
            action(k)
            return carry

        lax.fori_loop(1, n, step, 0)

    def split_index(index):
        whole = jnp.floor((index.astype(jnp.float32) + 0.5) * (1.0 / block))
        whole = whole.astype(jnp.int32)
        return whole, index - whole * block

    r = small[...]
    r_high = r.astype(jnp.bfloat16)
    r_low = (r - r_high.astype(jnp.float32)).astype(jnp.bfloat16)
    span = local // block

    def dot(a, b):
        return jnp.dot(a, b, preferred_element_type=jnp.float32)

    pieces, _, pw = pieced.shape
    inner = span // pieces

    def grid_of(shape, dim):
        return split_index(lax.broadcasted_iota(jnp.int32, shape, dim))

    def one_hot(hit):
        return jnp.where(hit, 1.0, 0.0).astype(jnp.bfloat16)

    col_p, col_q = grid_of((block, pw), 1)
    line = lax.broadcasted_iota(jnp.int32, (block, pw), 0)
    pick = one_hot(col_q == line)
    odd = jnp.zeros_like(line)
    for place in range(inner.bit_length()):
        odd = odd + ((line >> place) & 1) * ((col_p >> place) & 1)
    sign_right = jnp.where(line < inner, (1 - 2 * (odd & 1)).astype(jnp.float32), 0.0)
    row_p, row_q = grid_of((pw, block), 0)
    lane = lax.broadcasted_iota(jnp.int32, (pw, block), 1)
    left = one_hot(row_q == lane)
    sign = dot(one_hot(row_p == lane), sign_right.astype(jnp.bfloat16))
    high = (dot(left, dot(r_high, pick).astype(jnp.bfloat16)) * sign).astype(jnp.bfloat16)
    low = (dot(left, dot(r_low, pick).astype(jnp.bfloat16)) * sign).astype(jnp.bfloat16)
    for i in range(pieces):
        x = act[:, i * pw : (i + 1) * pw]
        pieced[i] = dot(x, high) + dot(x, low)

    def butterfly(values):
        stride = 1
        while stride < len(values):
            for at in range(len(values)):
                if not at & stride:
                    a, b = values[at], values[at + stride]
                    values[at], values[at + stride] = a + b, a - b
            stride *= 2
        return values

    for at in range(0, tokens, ROWS):
        values = butterfly([pieced[i, at : at + ROWS, :] for i in range(pieces)])
        own[at : at + ROWS, :] = jnp.concatenate(values, axis=1)
    pl.semaphore_wait(barrier, n - 1)
    for h in range(SPLIT):
        each(lambda k: out_copy(h, k).start())
        got[h, me] = own[rows_of(me, h * part), columns_of(me)]

    for h in range(SPLIT):
        each(lambda k: out_copy(h, k).wait_recv())
        for at in range(0, wide, LANES):
            for low in range(0, rows, ROWS):
                spot = (slice(low, low + ROWS), slice(at, at + LANES))
                values = butterfly([got[(h, s, *spot)] for s in range(n)])
                for s in range(n):
                    mixed[(h, s, *spot)] = values[s] * scale
        each(lambda k: back_copy(h, k).start())
        back[h, c, rows_of(me), :] = mixed[h, me]

    order = ends_first(nz)

    def place_of(i):
        return (1 - i % 2) * (nz - 1 - i // 2) + i % 2 * (i // 2)

    def owner(to, far, other):
        side = 1 - y if far else y
        return to * 4 + side * 2 + (1 - c if other else c)

    def core_copy(h, i, far):
        slot = (1 - far) * nz + i
        return remote(acc.at[h, owner(place_of(i), far, 1)], from_core.at[h, slot],
                      sa.at[h, slot], ra.at[h, slot], me + 1 - 2 * c)

    def y_copy(to, h):
        return remote(acc.at[h, owner(to, 1, 0)], from_y.at[to, h],
                      sb.at[to, h], rb.at[to, h], me + 2 * (1 - 2 * y))

    def up_copy(to, h, t):
        return remote(acc.at[h, t], from_low.at[to, h],
                      su.at[to, h], ru.at[to, h], lax.rem(me + 4, n))

    def down_copy(to, h, t):
        return remote(acc.at[h, t], from_high.at[to, h],
                      sd.at[to, h], rd.at[to, h], lax.rem(me + n - 4, n))

    def product(h, t):
        columns = pl.ds(pl.multiple_of(t * width, LANES), width)
        acc[h, t] = dot(rotated[h], w_v[:, columns])

    def loop(action):
        def step(i, carry):
            action(i)
            return carry

        lax.fori_loop(0, nz, step, 0)

    for h in range(SPLIT):
        each(lambda k: back_copy(h, k).wait_recv())
        rotated[h, :, :wide] = back[h, 0].astype(jnp.bfloat16)
        rotated[h, :, wide:] = back[h, 1, :, wide - shift :].astype(jnp.bfloat16)
        if h == 0:
            w_copy.wait()
        for far in (1, 0):
            def give(i):
                product(h, owner(place_of(i), far, 1))
                core_copy(h, i, far).start()

            loop(give)
        for far in (1, 0):
            def take(i):
                t = owner(place_of(i), far, 0)
                product(h, t)
                core_copy(h, i, far).wait_recv()
                acc[h, t] += from_core[h, (1 - far) * nz + i]
                if far:
                    y_copy(place_of(i), h).start()

            loop(take)

    for h in range(SPLIT):
        for to in order:
            t = owner(to, 0, 0)
            y_copy(to, h).wait_recv()
            acc[h, t] += from_y[to, h]

            @pl.when(z < to)
            def _():
                @pl.when(z > 0)
                def _():
                    up_copy(to, h, t).wait_recv()
                    acc[h, t] += from_low[to, h]

                up_copy(to, h, t).start()

            @pl.when(z > to)
            def _():
                @pl.when(z < nz - 1)
                def _():
                    down_copy(to, h, t).wait_recv()
                    acc[h, t] += from_high[to, h]

                down_copy(to, h, t).start()

    for h in range(SPLIT):
        @pl.when(z > 0)
        def _():
            up_copy(z, h, me).wait_recv()
            acc[h, me] += from_low[z, h]

        @pl.when(z < nz - 1)
        def _():
            down_copy(z, h, me).wait_recv()
            acc[h, me] += from_high[z, h]

        out[h * part : (h + 1) * part, :] = acc[h, me].astype(out.dtype)

    for h in range(SPLIT):
        each(lambda k: out_copy(h, k).wait_send())
        each(lambda k: back_copy(h, k).wait_send())
        for far in (1, 0):
            loop(lambda i: core_copy(h, i, far).wait_send())
        for to in order:
            t = owner(to, 0, 0)
            y_copy(to, h).wait_send()

            @pl.when(z < to)
            def _():
                up_copy(to, h, t).wait_send()

            @pl.when(z > to)
            def _():
                down_copy(to, h, t).wait_send()


def body(activations, rotation_small, down_weight):
    tokens, local = activations.shape
    n = lax.axis_size("tensor")
    features = down_weight.shape[1]
    block = rotation_small.shape[0]
    if n % 4 or block * block < local or tokens % (SPLIT * ROWS * (n // 2)) or local % LANES or features % (LANES * n):
        return plain(activations, rotation_small, down_weight)
    width, nz, part = features // n, n // 4, tokens // SPLIT
    rows = part // (n // 2)
    wide = -(-local // (2 * LANES)) * LANES
    pieces = 1
    while local // pieces > 2 * LANES and local // block % (2 * pieces) == 0:
        pieces *= 2
    f32 = jnp.float32
    dma = pltpu.SemaphoreType.DMA
    return pl.pallas_call(
        functools.partial(fused, n),
        out_shape=jax.ShapeDtypeStruct((tokens, width), jnp.bfloat16),
        in_specs=[
            pl.BlockSpec(memory_space=pltpu.VMEM),
            pl.BlockSpec(memory_space=pltpu.VMEM),
            pl.BlockSpec(memory_space=pl.ANY),
        ],
        out_specs=pl.BlockSpec(memory_space=pltpu.VMEM),
        scratch_shapes=[
            pltpu.VMEM((local, features), jnp.bfloat16),
            pltpu.VMEM((SPLIT, n, part, width), f32),
            pltpu.VMEM((pieces, tokens, local // pieces), f32),
            pltpu.VMEM((tokens, local), f32),
            pltpu.VMEM((SPLIT, n, rows, wide), f32),
            pltpu.VMEM((SPLIT, n, rows, wide), f32),
            pltpu.VMEM((SPLIT, 2, part, wide), f32),
            pltpu.VMEM((SPLIT, part, local), jnp.bfloat16),
            pltpu.VMEM((SPLIT, 2 * nz, part, width), f32),
            *[pltpu.VMEM((nz, SPLIT, part, width), f32)] * 3,
            dma(()),
            *[dma((SPLIT, n))] * 4,
            *[dma((SPLIT, 2 * nz))] * 2,
            *[dma((nz, SPLIT))] * 6,
        ],
        compiler_params=pltpu.CompilerParams(
            collective_id=0, has_side_effects=True, vmem_limit_bytes=60 * 2**20
        ),
    )(activations, rotation_small, down_weight)


def solution(mesh):
    placed = (P("groups", "tensor"), P(), P("tensor", None))
    return jax.shard_map(
        body, mesh=mesh, in_specs=placed, out_specs=P("groups", "tensor"), check_vma=False
    )
```

```python
import functools

import jax
import jax.numpy as jnp
from jax import lax
from jax.experimental import pallas as pl
from jax.experimental.pallas import tpu as pltpu
from jax.sharding import PartitionSpec as P

LANES = 128
ROWS = 8
SPLIT = 2


def sylvester(order):
    index = jnp.arange(order, dtype=jnp.int32)
    common = jnp.zeros((order, order), jnp.int32)
    for place in range(max(order.bit_length(), 1)):
        common = common + (index[:, None] >> place & 1) * (index[None, :] >> place & 1)
    return (1 - 2 * (common % 2)).astype(jnp.float32)


def plain(activations, rotation_small, down_weight):
    tokens, local = activations.shape
    shards = lax.axis_size("tensor")
    span = local // rotation_small.shape[0]
    kronecker = jnp.kron(sylvester(span), rotation_small)
    factor = (span * shards) ** (-0.5)
    values = activations.astype(jnp.float32)
    gathered = lax.all_to_all(values, "tensor", split_axis=0, concat_axis=1, tiled=True)
    gathered = gathered.reshape(-1, shards, local)
    gathered = jnp.einsum(
        "rsl,su->rul", gathered, sylvester(shards), precision=lax.Precision.HIGHEST
    )
    gathered = jnp.dot(gathered.reshape(-1, local), kronecker, precision=lax.Precision.HIGHEST)
    gathered = gathered.reshape(-1, shards * local)
    returned = lax.all_to_all(gathered, "tensor", split_axis=1, concat_axis=0, tiled=True)
    rotated = (returned * factor).astype(jnp.bfloat16)
    summed = lax.psum_scatter(
        lax.dot_general(
            down_weight, rotated, (((0,), (1,)), ((), ())), preferred_element_type=jnp.float32
        ),
        "tensor",
        scatter_dimension=0,
        tiled=True,
    )
    return summed.T.astype(jnp.bfloat16)


def ends_first(count):
    low, high, order = 0, count - 1, []
    while low <= high:
        order.append(high)
        if low < high:
            order.append(low)
        low, high = low + 1, high - 1
    return order


def fused(n, act, small, w_hbm, out, w_v, acc, pieced, own, got, mixed, back, rotated, from_core,
          from_y, from_low, from_high, w_sem, s1, r1, s2, r2, sa, ra, sb, rb, su, ru, sd, rd):
    tokens, local = act.shape
    block = small.shape[0]
    width = acc.shape[3]
    part = tokens // SPLIT
    rows = part // (n // 2)
    wide = got.shape[3]
    shift = local - wide
    nz = n // 4
    me = lax.axis_index("tensor")
    z, y, c = me // 4, (me // 2) % 2, me % 2
    scale = (local // block * n) ** (-0.5)
    w_copy = pltpu.make_async_copy(w_hbm, w_v, w_sem)
    w_copy.start()

    barrier = pltpu.get_barrier_semaphore()

    def greet(k, carry):
        pl.semaphore_signal(barrier, inc=1, device_id={"tensor": lax.rem(me + k, n)})
        return carry

    lax.fori_loop(1, n, greet, 0)

    def remote(src, dst, send, recv, to):
        return pltpu.make_async_remote_copy(
            src_ref=src, dst_ref=dst, send_sem=send, recv_sem=recv,
            device_id={"tensor": to}, device_id_type=pl.DeviceIdType.MESH,
        )

    def rows_of(rank, base=0):
        return pl.ds(pl.multiple_of(base + rank // 2 * rows, ROWS), rows)

    overlap = wide - shift
    first = -(-wide // (2 * LANES)) * LANES
    cuts = ((0, first), (first, wide - first))

    def columns_of(rank, q):
        return pl.ds(pl.multiple_of(rank % 2 * shift + cuts[q][0], LANES), cuts[q][1])

    def out_copy(h, q, k):
        to = lax.rem(me + k, n)
        return remote(own.at[rows_of(to, h * part), columns_of(to, q)],
                      got.at[h, me, :, pl.ds(*cuts[q])], s1.at[h, q, k], r1.at[h, q, k], to)

    def back_copy(h, q, k):
        to = lax.rem(me + k, n)
        return remote(mixed.at[h, to, :, pl.ds(*cuts[q])],
                      back.at[h, c, rows_of(me), pl.ds(*cuts[q])],
                      s2.at[h, q, k], r2.at[h, q, k], to)

    def each(action):
        def step(k, carry):
            action(k)
            return carry

        lax.fori_loop(1, n, step, 0)

    def split_index(index):
        whole = jnp.floor((index.astype(jnp.float32) + 0.5) * (1.0 / block))
        whole = whole.astype(jnp.int32)
        return whole, index - whole * block

    r = small[...]
    r_high = r.astype(jnp.bfloat16)
    r_low = (r - r_high.astype(jnp.float32)).astype(jnp.bfloat16)
    span = local // block

    def dot(a, b):
        return jnp.dot(a, b, preferred_element_type=jnp.float32)

    pieces, _, pw = pieced.shape
    inner = span // pieces

    def grid_of(shape, dim):
        return split_index(lax.broadcasted_iota(jnp.int32, shape, dim))

    def one_hot(hit):
        return jnp.where(hit, 1.0, 0.0).astype(jnp.bfloat16)

    col_p, col_q = grid_of((block, pw), 1)
    line = lax.broadcasted_iota(jnp.int32, (block, pw), 0)
    pick = one_hot(col_q == line)
    odd = jnp.zeros_like(line)
    for place in range(inner.bit_length()):
        odd = odd + ((line >> place) & 1) * ((col_p >> place) & 1)
    sign_right = jnp.where(line < inner, (1 - 2 * (odd & 1)).astype(jnp.float32), 0.0)
    row_p, row_q = grid_of((pw, block), 0)
    lane = lax.broadcasted_iota(jnp.int32, (pw, block), 1)
    left = one_hot(row_q == lane)
    sign = dot(one_hot(row_p == lane), sign_right.astype(jnp.bfloat16))
    high = (dot(left, dot(r_high, pick).astype(jnp.bfloat16)) * sign).astype(jnp.bfloat16)
    low = (dot(left, dot(r_low, pick).astype(jnp.bfloat16)) * sign).astype(jnp.bfloat16)
    for i in range(pieces):
        x = act[:, i * pw : (i + 1) * pw]
        pieced[i] = dot(x, high) + dot(x, low)

    def butterfly(values):
        stride = 1
        while stride < len(values):
            for at in range(len(values)):
                if not at & stride:
                    a, b = values[at], values[at + stride]
                    values[at], values[at + stride] = a + b, a - b
            stride *= 2
        return values

    for at in range(0, tokens, ROWS):
        values = butterfly([pieced[i, at : at + ROWS, :] for i in range(pieces)])
        own[at : at + ROWS, :] = jnp.concatenate(values, axis=1)
    pl.semaphore_wait(barrier, n - 1)
    stages = [(h, q) for h in range(SPLIT) for q in range(2)]
    for h, q in stages:
        each(lambda k: out_copy(h, q, k).start())
        got[h, me, :, pl.ds(*cuts[q])] = own[rows_of(me, h * part), columns_of(me, q)]

    for h, q in stages:
        each(lambda k: out_copy(h, q, k).wait_recv())
        for at in range(cuts[q][0], sum(cuts[q]), LANES):
            for low in range(0, rows, ROWS):
                spot = (slice(low, low + ROWS), slice(at, at + LANES))
                values = butterfly([got[(h, s, *spot)] for s in range(n)])
                for s in range(n):
                    mixed[(h, s, *spot)] = values[s] * scale
        each(lambda k: back_copy(h, q, k).start())
        back[h, c, rows_of(me), pl.ds(*cuts[q])] = mixed[h, me, :, pl.ds(*cuts[q])]

    order = ends_first(nz)

    def place_of(i):
        return (1 - i % 2) * (nz - 1 - i // 2) + i % 2 * (i // 2)

    def owner(to, far, other):
        side = 1 - y if far else y
        return to * 4 + side * 2 + (1 - c if other else c)

    def core_copy(h, i, far):
        slot = (1 - far) * nz + i
        return remote(acc.at[h, owner(place_of(i), far, 1)], from_core.at[h, slot],
                      sa.at[h, slot], ra.at[h, slot], me + 1 - 2 * c)

    def y_copy(to, h):
        return remote(acc.at[h, owner(to, 1, 0)], from_y.at[to, h],
                      sb.at[to, h], rb.at[to, h], me + 2 * (1 - 2 * y))

    def up_copy(to, h, t):
        return remote(acc.at[h, t], from_low.at[to, h],
                      su.at[to, h], ru.at[to, h], lax.rem(me + 4, n))

    def down_copy(to, h, t):
        return remote(acc.at[h, t], from_high.at[to, h],
                      sd.at[to, h], rd.at[to, h], lax.rem(me + n - 4, n))

    def spans(q):
        at, size = cuts[q]
        low = max(at, overlap)
        return (0, at, size), (1, low, at + size - low)

    def receive(h, q):
        each(lambda k: back_copy(h, q, k).wait_recv())
        for side, at, size in spans(q):
            rotated[h, :, pl.ds(side * shift + at, size)] = (
                back[h, side, :, pl.ds(at, size)].astype(jnp.bfloat16)
            )

    def product(h, q, t):
        columns = pl.ds(pl.multiple_of(t * width, LANES), width)
        terms = [
            dot(rotated[h, :, pl.ds(side * shift + at, size)],
                w_v[pl.ds(side * shift + at, size), columns])
            for side, at, size in spans(q)
        ]
        return terms[0] + terms[1]

    def loop(count, action):
        def step(i, carry):
            action(i)
            return carry

        lax.fori_loop(0, count, step, 0)

    def begin(h):
        receive(h, 0)
        if h == 0:
            w_copy.wait()

        def tile(t):
            acc[h, t] = product(h, 0, t)

        loop(n, tile)
        receive(h, 1)

    def give(h, far, i):
        t = owner(place_of(i), far, 1)
        acc[h, t] += product(h, 1, t)
        core_copy(h, i, far).start()

    def take(h, far, i):
        t = owner(place_of(i), far, 0)
        acc[h, t] += product(h, 1, t)
        core_copy(h, i, far).wait_recv()
        acc[h, t] += from_core[h, (1 - far) * nz + i]
        if far:
            y_copy(place_of(i), h).start()

    def pass_on(h, to):
        t = owner(to, 0, 0)
        y_copy(to, h).wait_recv()
        acc[h, t] += from_y[to, h]

        @pl.when(z < to)
        def _():
            @pl.when(z > 0)
            def _():
                up_copy(to, h, t).wait_recv()
                acc[h, t] += from_low[to, h]

            up_copy(to, h, t).start()

        @pl.when(z > to)
        def _():
            @pl.when(z < nz - 1)
            def _():
                down_copy(to, h, t).wait_recv()
                acc[h, t] += from_high[to, h]

            down_copy(to, h, t).start()

    for h in range(SPLIT):
        begin(h)
        loop(nz, lambda i: give(h, 1, i))
        loop(nz, lambda i: take(h, 1, i))
        for i, to in enumerate(order):
            if h:
                pass_on(h - 1, to)
            give(h, 0, i)
        loop(nz, lambda i: take(h, 0, i))
    for to in order:
        pass_on(SPLIT - 1, to)

    for h in range(SPLIT):
        @pl.when(z > 0)
        def _():
            up_copy(z, h, me).wait_recv()
            acc[h, me] += from_low[z, h]

        @pl.when(z < nz - 1)
        def _():
            down_copy(z, h, me).wait_recv()
            acc[h, me] += from_high[z, h]

        out[h * part : (h + 1) * part, :] = acc[h, me].astype(out.dtype)

    for h in range(SPLIT):
        for q in range(2):
            each(lambda k: out_copy(h, q, k).wait_send())
            each(lambda k: back_copy(h, q, k).wait_send())
        for far in (1, 0):
            loop(nz, lambda i: core_copy(h, i, far).wait_send())
        for to in order:
            t = owner(to, 0, 0)
            y_copy(to, h).wait_send()

            @pl.when(z < to)
            def _():
                up_copy(to, h, t).wait_send()

            @pl.when(z > to)
            def _():
                down_copy(to, h, t).wait_send()


def body(activations, rotation_small, down_weight):
    tokens, local = activations.shape
    n = lax.axis_size("tensor")
    features = down_weight.shape[1]
    block = rotation_small.shape[0]
    if n % 4 or block * block < local or tokens % (SPLIT * ROWS * (n // 2)) or local % LANES or features % (LANES * n):
        return plain(activations, rotation_small, down_weight)
    width, nz, part = features // n, n // 4, tokens // SPLIT
    rows = part // (n // 2)
    wide = -(-local // (2 * LANES)) * LANES
    pieces = 1
    while local // pieces > 2 * LANES and local // block % (2 * pieces) == 0:
        pieces *= 2
    f32 = jnp.float32
    dma = pltpu.SemaphoreType.DMA
    return pl.pallas_call(
        functools.partial(fused, n),
        out_shape=jax.ShapeDtypeStruct((tokens, width), jnp.bfloat16),
        in_specs=[
            pl.BlockSpec(memory_space=pltpu.VMEM),
            pl.BlockSpec(memory_space=pltpu.VMEM),
            pl.BlockSpec(memory_space=pl.ANY),
        ],
        out_specs=pl.BlockSpec(memory_space=pltpu.VMEM),
        scratch_shapes=[
            pltpu.VMEM((local, features), jnp.bfloat16),
            pltpu.VMEM((SPLIT, n, part, width), f32),
            pltpu.VMEM((pieces, tokens, local // pieces), f32),
            pltpu.VMEM((tokens, local), f32),
            pltpu.VMEM((SPLIT, n, rows, wide), f32),
            pltpu.VMEM((SPLIT, n, rows, wide), f32),
            pltpu.VMEM((SPLIT, 2, part, wide), f32),
            pltpu.VMEM((SPLIT, part, local), jnp.bfloat16),
            pltpu.VMEM((SPLIT, 2 * nz, part, width), f32),
            *[pltpu.VMEM((nz, SPLIT, part, width), f32)] * 3,
            dma(()),
            *[dma((SPLIT, 2, n))] * 4,
            *[dma((SPLIT, 2 * nz))] * 2,
            *[dma((nz, SPLIT))] * 6,
        ],
        compiler_params=pltpu.CompilerParams(
            collective_id=0, has_side_effects=True, vmem_limit_bytes=60 * 2**20
        ),
    )(activations, rotation_small, down_weight)


def solution(mesh):
    placed = (P("groups", "tensor"), P(), P("tensor", None))
    return jax.shard_map(
        body, mesh=mesh, in_specs=placed, out_specs=P("groups", "tensor"), check_vma=False
    )
```

```python
import functools

import jax
import jax.numpy as jnp
from jax import lax
from jax.experimental import pallas as pl
from jax.experimental.pallas import tpu as pltpu
from jax.sharding import PartitionSpec as P

LANES = 128
ROWS = 8
SPLIT = 2


def sylvester(order):
    index = jnp.arange(order, dtype=jnp.int32)
    common = jnp.zeros((order, order), jnp.int32)
    for place in range(max(order.bit_length(), 1)):
        common = common + (index[:, None] >> place & 1) * (index[None, :] >> place & 1)
    return (1 - 2 * (common % 2)).astype(jnp.float32)


def plain(activations, rotation_small, down_weight):
    tokens, local = activations.shape
    shards = lax.axis_size("tensor")
    span = local // rotation_small.shape[0]
    kronecker = jnp.kron(sylvester(span), rotation_small)
    factor = (span * shards) ** (-0.5)
    values = activations.astype(jnp.float32)
    gathered = lax.all_to_all(values, "tensor", split_axis=0, concat_axis=1, tiled=True)
    gathered = gathered.reshape(-1, shards, local)
    gathered = jnp.einsum(
        "rsl,su->rul", gathered, sylvester(shards), precision=lax.Precision.HIGHEST
    )
    gathered = jnp.dot(gathered.reshape(-1, local), kronecker, precision=lax.Precision.HIGHEST)
    gathered = gathered.reshape(-1, shards * local)
    returned = lax.all_to_all(gathered, "tensor", split_axis=1, concat_axis=0, tiled=True)
    rotated = (returned * factor).astype(jnp.bfloat16)
    summed = lax.psum_scatter(
        lax.dot_general(
            down_weight, rotated, (((0,), (1,)), ((), ())), preferred_element_type=jnp.float32
        ),
        "tensor",
        scatter_dimension=0,
        tiled=True,
    )
    return summed.T.astype(jnp.bfloat16)


def ends_first(count):
    low, high, order = 0, count - 1, []
    while low <= high:
        order.append(high)
        if low < high:
            order.append(low)
        low, high = low + 1, high - 1
    return order


def fused(n, act, small, w_hbm, out, w_v, acc, pieced, own, got, mixed, back, rotated, from_core,
          from_y, from_low, from_high, w_sem, s1, r1, s2, r2, sa, ra, sb, rb, su, ru, sd, rd):
    tokens, local = act.shape
    block = small.shape[0]
    width = acc.shape[3]
    part = tokens // SPLIT
    rows = part // (n // 2)
    wide = got.shape[3]
    shift = local - wide
    nz = n // 4
    me = lax.axis_index("tensor")
    z, y, c = me // 4, (me // 2) % 2, me % 2
    scale = (local // block * n) ** (-0.5)
    w_copy = pltpu.make_async_copy(w_hbm, w_v, w_sem)
    w_copy.start()

    barrier = pltpu.get_barrier_semaphore()

    def greet(k, carry):
        pl.semaphore_signal(barrier, inc=1, device_id={"tensor": lax.rem(me + k, n)})
        return carry

    lax.fori_loop(1, n, greet, 0)

    def remote(src, dst, send, recv, to):
        return pltpu.make_async_remote_copy(
            src_ref=src, dst_ref=dst, send_sem=send, recv_sem=recv,
            device_id={"tensor": to}, device_id_type=pl.DeviceIdType.MESH,
        )

    def rows_of(rank, base=0):
        return pl.ds(pl.multiple_of(base + rank // 2 * rows, ROWS), rows)

    overlap = wide - shift
    cuts = ((0, wide),)

    def columns_of(rank, q):
        return pl.ds(pl.multiple_of(rank % 2 * shift + cuts[q][0], LANES), cuts[q][1])

    def out_copy(h, q, k):
        to = lax.rem(me + k, n)
        return remote(own.at[rows_of(to, h * part), columns_of(to, q)],
                      got.at[h, me, :, pl.ds(*cuts[q])], s1.at[h, q, k], r1.at[h, q, k], to)

    def back_copy(h, q, k):
        to = lax.rem(me + k, n)
        return remote(mixed.at[h, to, :, pl.ds(*cuts[q])],
                      back.at[h, c, rows_of(me), pl.ds(*cuts[q])],
                      s2.at[h, q, k], r2.at[h, q, k], to)

    def each(action):
        def step(k, carry):
            action(k)
            return carry

        lax.fori_loop(1, n, step, 0)

    def split_index(index):
        whole = jnp.floor((index.astype(jnp.float32) + 0.5) * (1.0 / block))
        whole = whole.astype(jnp.int32)
        return whole, index - whole * block

    r = small[...]
    r_high = r.astype(jnp.bfloat16)
    r_low = (r - r_high.astype(jnp.float32)).astype(jnp.bfloat16)
    span = local // block

    def dot(a, b):
        return jnp.dot(a, b, preferred_element_type=jnp.float32)

    pieces, _, pw = pieced.shape
    inner = span // pieces

    def grid_of(shape, dim):
        return split_index(lax.broadcasted_iota(jnp.int32, shape, dim))

    def one_hot(hit):
        return jnp.where(hit, 1.0, 0.0).astype(jnp.bfloat16)

    col_p, col_q = grid_of((block, pw), 1)
    line = lax.broadcasted_iota(jnp.int32, (block, pw), 0)
    pick = one_hot(col_q == line)
    odd = jnp.zeros_like(line)
    for place in range(inner.bit_length()):
        odd = odd + ((line >> place) & 1) * ((col_p >> place) & 1)
    sign_right = jnp.where(line < inner, (1 - 2 * (odd & 1)).astype(jnp.float32), 0.0)
    row_p, row_q = grid_of((pw, block), 0)
    lane = lax.broadcasted_iota(jnp.int32, (pw, block), 1)
    left = one_hot(row_q == lane)
    sign = dot(one_hot(row_p == lane), sign_right.astype(jnp.bfloat16))
    high = (dot(left, dot(r_high, pick).astype(jnp.bfloat16)) * sign).astype(jnp.bfloat16)
    low = (dot(left, dot(r_low, pick).astype(jnp.bfloat16)) * sign).astype(jnp.bfloat16)
    for i in range(pieces):
        x = act[:, i * pw : (i + 1) * pw]
        pieced[i] = dot(x, high) + dot(x, low)

    def butterfly(values):
        stride = 1
        while stride < len(values):
            for at in range(len(values)):
                if not at & stride:
                    a, b = values[at], values[at + stride]
                    values[at], values[at + stride] = a + b, a - b
            stride *= 2
        return values

    for at in range(0, tokens, ROWS):
        values = butterfly([pieced[i, at : at + ROWS, :] for i in range(pieces)])
        own[at : at + ROWS, :] = jnp.concatenate(values, axis=1)
    pl.semaphore_wait(barrier, n - 1)
    stages = [(h, q) for h in range(SPLIT) for q in range(len(cuts))]
    for h, q in stages:
        each(lambda k: out_copy(h, q, k).start())
        got[h, me, :, pl.ds(*cuts[q])] = own[rows_of(me, h * part), columns_of(me, q)]

    for h, q in stages:
        each(lambda k: out_copy(h, q, k).wait_recv())
        for at in range(cuts[q][0], sum(cuts[q]), LANES):
            for low in range(0, rows, ROWS):
                spot = (slice(low, low + ROWS), slice(at, at + LANES))
                values = butterfly([got[(h, s, *spot)] for s in range(n)])
                for s in range(n):
                    mixed[(h, s, *spot)] = values[s] * scale
        each(lambda k: back_copy(h, q, k).start())
        back[h, c, rows_of(me), pl.ds(*cuts[q])] = mixed[h, me, :, pl.ds(*cuts[q])]

    order = ends_first(nz)

    def place_of(i):
        return (1 - i % 2) * (nz - 1 - i // 2) + i % 2 * (i // 2)

    def owner(to, far, other):
        side = 1 - y if far else y
        return to * 4 + side * 2 + (1 - c if other else c)

    def core_copy(h, i, far):
        slot = (1 - far) * nz + i
        return remote(acc.at[h, owner(place_of(i), far, 1)], from_core.at[h, slot],
                      sa.at[h, slot], ra.at[h, slot], me + 1 - 2 * c)

    def y_copy(to, h):
        return remote(acc.at[h, owner(to, 1, 0)], from_y.at[to, h],
                      sb.at[to, h], rb.at[to, h], me + 2 * (1 - 2 * y))

    def up_copy(to, h, t):
        return remote(acc.at[h, t], from_low.at[to, h],
                      su.at[to, h], ru.at[to, h], lax.rem(me + 4, n))

    def down_copy(to, h, t):
        return remote(acc.at[h, t], from_high.at[to, h],
                      sd.at[to, h], rd.at[to, h], lax.rem(me + n - 4, n))

    def spans(q):
        at, size = cuts[q]
        low = max(at, overlap)
        return (0, at, size), (1, low, at + size - low)

    def receive(h, q):
        each(lambda k: back_copy(h, q, k).wait_recv())
        for side, at, size in spans(q):
            rotated[h, :, pl.ds(side * shift + at, size)] = (
                back[h, side, :, pl.ds(at, size)].astype(jnp.bfloat16)
            )

    def product(h, t):
        columns = pl.ds(pl.multiple_of(t * width, LANES), width)
        return dot(rotated[h], w_v[:, columns])

    def loop(count, action):
        def step(i, carry):
            action(i)
            return carry

        lax.fori_loop(0, count, step, 0)

    def begin(h):
        receive(h, 0)
        if h == 0:
            w_copy.wait()

    def give(h, far, i):
        t = owner(place_of(i), far, 1)
        acc[h, t] = product(h, t)
        core_copy(h, i, far).start()

    def take(h, far, i):
        t = owner(place_of(i), far, 0)
        acc[h, t] = product(h, t)
        core_copy(h, i, far).wait_recv()
        acc[h, t] += from_core[h, (1 - far) * nz + i]
        if far:
            y_copy(place_of(i), h).start()

    def pass_on(h, to):
        t = owner(to, 0, 0)
        y_copy(to, h).wait_recv()
        acc[h, t] += from_y[to, h]

        @pl.when(z < to)
        def _():
            @pl.when(z > 0)
            def _():
                up_copy(to, h, t).wait_recv()
                acc[h, t] += from_low[to, h]

            up_copy(to, h, t).start()

        @pl.when(z > to)
        def _():
            @pl.when(z < nz - 1)
            def _():
                down_copy(to, h, t).wait_recv()
                acc[h, t] += from_high[to, h]

            down_copy(to, h, t).start()

    for h in range(SPLIT):
        begin(h)
        loop(nz, lambda i: give(h, 1, i))
        loop(nz, lambda i: take(h, 1, i))
        for i, to in enumerate(order):
            if h:
                pass_on(h - 1, to)
            give(h, 0, i)
        loop(nz, lambda i: take(h, 0, i))
    for to in order:
        pass_on(SPLIT - 1, to)

    for h in range(SPLIT):
        @pl.when(z > 0)
        def _():
            up_copy(z, h, me).wait_recv()
            acc[h, me] += from_low[z, h]

        @pl.when(z < nz - 1)
        def _():
            down_copy(z, h, me).wait_recv()
            acc[h, me] += from_high[z, h]

        out[h * part : (h + 1) * part, :] = acc[h, me].astype(out.dtype)

    for h in range(SPLIT):
        for q in range(len(cuts)):
            each(lambda k: out_copy(h, q, k).wait_send())
            each(lambda k: back_copy(h, q, k).wait_send())
        for far in (1, 0):
            loop(nz, lambda i: core_copy(h, i, far).wait_send())
        for to in order:
            t = owner(to, 0, 0)
            y_copy(to, h).wait_send()

            @pl.when(z < to)
            def _():
                up_copy(to, h, t).wait_send()

            @pl.when(z > to)
            def _():
                down_copy(to, h, t).wait_send()


def body(activations, rotation_small, down_weight):
    tokens, local = activations.shape
    n = lax.axis_size("tensor")
    features = down_weight.shape[1]
    block = rotation_small.shape[0]
    if n % 4 or block * block < local or tokens % (SPLIT * ROWS * (n // 2)) or local % LANES or features % (LANES * n):
        return plain(activations, rotation_small, down_weight)
    width, nz, part = features // n, n // 4, tokens // SPLIT
    rows = part // (n // 2)
    wide = -(-local // (2 * LANES)) * LANES
    pieces = 1
    while local // pieces > 2 * LANES and local // block % (2 * pieces) == 0:
        pieces *= 2
    f32 = jnp.float32
    dma = pltpu.SemaphoreType.DMA
    return pl.pallas_call(
        functools.partial(fused, n),
        out_shape=jax.ShapeDtypeStruct((tokens, width), jnp.bfloat16),
        in_specs=[
            pl.BlockSpec(memory_space=pltpu.VMEM),
            pl.BlockSpec(memory_space=pltpu.VMEM),
            pl.BlockSpec(memory_space=pl.ANY),
        ],
        out_specs=pl.BlockSpec(memory_space=pltpu.VMEM),
        scratch_shapes=[
            pltpu.VMEM((local, features), jnp.bfloat16),
            pltpu.VMEM((SPLIT, n, part, width), f32),
            pltpu.VMEM((pieces, tokens, local // pieces), f32),
            pltpu.VMEM((tokens, local), f32),
            pltpu.VMEM((SPLIT, n, rows, wide), f32),
            pltpu.VMEM((SPLIT, n, rows, wide), f32),
            pltpu.VMEM((SPLIT, 2, part, wide), f32),
            pltpu.VMEM((SPLIT, part, local), jnp.bfloat16),
            pltpu.VMEM((SPLIT, 2 * nz, part, width), f32),
            *[pltpu.VMEM((nz, SPLIT, part, width), f32)] * 3,
            dma(()),
            *[dma((SPLIT, 1, n))] * 4,
            *[dma((SPLIT, 2 * nz))] * 2,
            *[dma((nz, SPLIT))] * 6,
        ],
        compiler_params=pltpu.CompilerParams(
            collective_id=0, has_side_effects=True, vmem_limit_bytes=60 * 2**20
        ),
    )(activations, rotation_small, down_weight)


def solution(mesh):
    placed = (P("groups", "tensor"), P(), P("tensor", None))
    return jax.shard_map(
        body, mesh=mesh, in_specs=placed, out_specs=P("groups", "tensor"), check_vma=False
    )
```
